256 devices in a mesh: tile: 128 (over x, y, z), rep: 2 (over core).
Axes of the slice: x: 4, y: 4, z: 8, core: 2. Of those that a mesh axis runs over, the one named last changes fastest.
Arguments:
- amplitudes: bfloat16 [2048, 128, 1024], P('tile', None, 'rep'), may hold values from -6 to 6
- integrals: bfloat16 [384, 1024, 1024], P('tile'), may hold values from -0.1875 to 0.1875
- task_cd: int32 [384], P('tile'), may hold values from 0 to 127
- task_ab: int32 [384], P('tile'), may hold values from 0 to 63
- task_allowed: int32 [384], P('tile'), may hold values from 0 to 1, as said below
- mirror: int32 [2048], P(('tile', 'rep')), may hold values from 0 to 2047, as said below
- residual_in: bfloat16 [2048, 64, 1024], P(('tile', 'rep')), may hold values from -6 to 6
Outputs:
- residual_out: bfloat16 [2048, 64, 1024], P(('tile', 'rep'))
The draws below stay inside these ranges and needn't reach their ends.
Inputs may be any that keep to these rules, and one draw needn't show every extreme that they name: `task_allowed`: in each aligned block of 3 slots (the slots of one device along tile) one to 2 slots are allowed; some block has exactly 2. mirror is an involution on the occupied pairs without fixed points. Split the pairs into aligned blocks of 8; for b < 128, mirror maps block b one to one onto block b + 128.
All inputs are finite; a program needn't handle non-finite values.
Results may differ from the reference program's by a relative error of at most 0.0055.
Values may be sent and summed in bfloat16 or wider, within the bound.
A program may use at most 128 MiB of HBM per device.

```python
import jax
import jax.numpy as jnp
from jax import lax

ABW = 1024
CDW = 1024
ROWS_DEV = 16
TASK_DEV = 3
LIVE_MAX = 2
IJ = 2048
NCD = 128
NAB = 64
TASKS = 384


def draw_task_allowed(key, part):
    device_count = NAB * 2
    key_counts, key_busy, key_order = jax.random.split(key, 3)
    counts = jax.random.randint(key_counts, (device_count,), 1, LIVE_MAX + 1)
    busiest = jax.random.randint(key_busy, (), 0, device_count)
    counts = jnp.where(jnp.arange(device_count) == busiest, LIVE_MAX, counts)
    scores = jax.random.randint(key_order, (device_count, TASK_DEV), 0, 1 << 20) * TASK_DEV + jnp.arange(TASK_DEV)[None, :]
    ranking = jnp.argsort(jnp.argsort(scores, axis=1), axis=1)
    return (ranking < counts[:, None]).astype(jnp.int32).reshape(-1)


def draw_mirror(key, part):
    device_count = NAB * 2
    half_rows = ROWS_DEV // 2
    scores = jax.random.randint(key, (device_count, half_rows), 0, 1 << 20) * half_rows + jnp.arange(half_rows)[None, :]
    forward = jnp.argsort(scores, axis=1).astype(jnp.int32)
    backward = jnp.argsort(forward, axis=1).astype(jnp.int32)
    block_start = jnp.arange(device_count, dtype=jnp.int32)[:, None] * half_rows
    lower_rows = (block_start + device_count * half_rows + forward).reshape(-1)
    upper_rows = (block_start + backward).reshape(-1)
    return jnp.concatenate([lower_rows, upper_rows]).astype(jnp.int32)


def set_ends(array, key, least, high):
    longest = array.shape.index(max(array.shape))
    spots = []
    for shift in (0, 1):
        where = [jax.random.randint(jax.random.fold_in(key, axis), (), 0, length) for axis, length in enumerate(array.shape)]
        where[longest] = (where[longest] + shift) % array.shape[longest]
        spots.append(tuple(where))
    return array.at[spots[0]].set(least).at[spots[1]].set(high)


def levels(own_key, shape, shards, low, high):
    gain = 1.0
    for position, blocks in shards:
        heights = jax.random.uniform(jax.random.fold_in(jax.random.fold_in(own_key, 6), position), (blocks,), jnp.float32, low / len(shards), high / len(shards))
        gain = gain * jnp.repeat(jnp.exp(heights), shape[position] // blocks).reshape((-1,) + (1,) * (len(shape) - 1 - position))
    return gain


def gaussian(own_key, extent, deviation, most, shards=(), kind=jnp.bfloat16):
    result = jax.random.normal(own_key, extent, jnp.float32) * deviation
    if len(shards) > 0:
        result = levels(own_key, extent, shards, -0.22, 0.18) * result
    return jnp.clip(result, min=-most, max=most).astype(kind)


def setup_inputs(seed: int = 0) -> dict:
    splits = jax.random.split(jax.random.key(seed), 8)
    return {
        "amplitudes": gaussian(splits[0], (IJ, NCD, CDW), 1.0, 6.0, ((0, 128), (2, 2))),
        "integrals": gaussian(splits[1], (TASKS, ABW, CDW), CDW ** -0.5, 0.1875, ((0, 128),)),
        "task_cd": set_ends(jax.random.randint(splits[2], (TASKS,), 0, NCD), jax.random.fold_in(splits[2], 1), 0, NCD - 1).astype(jnp.int32),
        "task_ab": set_ends(jax.random.randint(splits[3], (TASKS,), 0, NAB), jax.random.fold_in(splits[3], 1), 0, NAB - 1).astype(jnp.int32),
        "task_allowed": draw_task_allowed(jax.random.fold_in(splits[7], 71), 0),
        "mirror": draw_mirror(jax.random.fold_in(splits[7], 71), 0),
        "residual_in": gaussian(splits[6], (IJ, NAB, ABW), 1.0, 6.0, ((0, 256),)),
    }


def reference(amplitudes, integrals, task_cd, task_ab, task_allowed, mirror, residual_in):
    half_width = amplitudes.shape[2] // 2

    def add_task(running, task_item):
        cd_tile, ab_tile, allowed, integral = task_item
        columns = lax.dynamic_index_in_dim(amplitudes, cd_tile, axis=1, keepdims=False)
        lower_half = jnp.dot(columns[:, :half_width], integral[:, :half_width].T, preferred_element_type=jnp.float32).astype(jnp.bfloat16)
        upper_half = jnp.dot(columns[:, half_width:], integral[:, half_width:].T, preferred_element_type=jnp.float32).astype(jnp.bfloat16)
        lower_half, upper_half = lax.optimization_barrier((lower_half, upper_half))
        combined = (lower_half.astype(jnp.float32) + upper_half.astype(jnp.float32)).astype(jnp.bfloat16)
        combined = lax.optimization_barrier(combined)
        weighted = combined.astype(jnp.float32) * allowed.astype(jnp.float32)
        current = lax.dynamic_index_in_dim(running, ab_tile, axis=1, keepdims=False)
        running = lax.dynamic_update_index_in_dim(running, current + weighted, ab_tile, axis=1)
        return running, None

    start_value = jnp.zeros((IJ, NAB, ABW), jnp.float32)
    ladder, _ = lax.scan(add_task, start_value, (task_cd, task_ab, task_allowed, integrals))
    summed = residual_in.astype(jnp.float32) + ladder
    mirrored = jnp.take(summed, mirror, axis=0)
    return (0.5 * (summed - mirrored)).astype(jnp.bfloat16)
```

```python
import jax
import jax.numpy as jnp
from jax import lax
from jax.sharding import PartitionSpec as P

BOTH = ("tile", "rep")


def partner_2(shard, axis, bit):
    return lax.ppermute(shard, axis, [(i, i ^ 1 << bit) for i in range(lax.axis_size(axis))])


def per_device(amplitudes, integrals, task_cd, task_ab, task_allowed, mirror, residual_in):
    peer_count = lax.axis_size("tile")
    rep_count = lax.axis_size("rep")
    rows_own, _, half_cols = amplitudes.shape
    local_rows = residual_in.shape[0]
    tile_width = integrals.shape[1]
    rep = lax.axis_index("rep")

    order = jnp.argsort(1 - task_allowed, stable=True)
    slot = order[rep]
    mine = jnp.stack([task_cd[slot], task_ab[slot], task_allowed[slot]])
    every = lax.all_gather(mine, BOTH, axis=0, tiled=False)
    every_cd, every_ab, every_allowed = every[:, 0], every[:, 1], every[:, 2]

    outgoing = jnp.take(amplitudes, every_cd, axis=1)
    incoming = lax.all_to_all(outgoing, BOTH, split_axis=1, concat_axis=0, tiled=True)
    incoming = incoming.reshape(peer_count, rep_count, rows_own, half_cols)
    integral = lax.dynamic_index_in_dim(integrals, slot, axis=0, keepdims=False)
    integral = integral.reshape(tile_width, rep_count, half_cols)
    halves = jnp.einsum(
        "tric,arc->rtia", incoming, integral, preferred_element_type=jnp.float32
    ).astype(jnp.bfloat16)

    contribution = (halves[0].astype(jnp.float32) + halves[1].astype(jnp.float32)).astype(
        jnp.bfloat16
    )
    contribution = contribution.reshape(peer_count * rep_count, local_rows, tile_width)
    arrived = lax.all_to_all(contribution, BOTH, split_axis=0, concat_axis=0, tiled=True)

    tile_ids = jnp.arange(residual_in.shape[1], dtype=jnp.int32)
    weights = ((every_ab[:, None] == tile_ids[None, :]) & (every_allowed[:, None] == 1)).astype(
        jnp.bfloat16
    )
    ladder = jnp.einsum("qa,qrc->rac", weights, arrived, preferred_element_type=jnp.float32)
    summed = residual_in.astype(jnp.float32) + ladder
    partner = partner_2(summed, "tile", peer_count.bit_length() - 2)
    mirrored = jnp.take(partner, mirror % local_rows, axis=0)
    return (0.5 * (summed - mirrored)).astype(jnp.bfloat16)

def solution(mesh):
    return jax.shard_map(
        per_device,
        mesh=mesh,
        in_specs=(
            P("tile", None, "rep"),
            P("tile", None, None),
            P("tile"),
            P("tile"),
            P("tile"),
            P(("tile", "rep")),
            P(("tile", "rep"), None, None),
        ),
        out_specs=P(("tile", "rep"), None, None),
        check_vma=False,
    )
```

```python
import jax
import jax.numpy as jnp
from jax import lax
from jax.sharding import PartitionSpec as P

BOTH = ("tile", "rep")


def partner_2(shard, axis, bit):
    return lax.ppermute(shard, axis, [(i, i ^ 1 << bit) for i in range(lax.axis_size(axis))])


def per_device(amplitudes, integrals, task_cd, task_ab, task_allowed, mirror, residual_in):
    peer_count = lax.axis_size("tile")
    rep_count = lax.axis_size("rep")
    rows_own, _, half_cols = amplitudes.shape
    local_rows = residual_in.shape[0]
    tile_width = integrals.shape[1]
    rep = lax.axis_index("rep")

    half_pairs = peer_count * rep_count // 2
    upper = lax.axis_index("tile") >= peer_count // 2
    partner_res = partner_2(residual_in, "tile", peer_count.bit_length() - 2)

    order = jnp.argsort(1 - task_allowed, stable=True)
    slot = order[rep]
    mine = jnp.concatenate([jnp.stack([task_cd[slot], task_ab[slot], task_allowed[slot]]), mirror])
    every = lax.all_gather(mine.astype(jnp.float32), BOTH, axis=0, tiled=False).astype(jnp.int32)
    every_cd, every_ab, every_allowed = every[:, 0], every[:, 1], every[:, 2]
    lower_mirror = every[:half_pairs, 3:].reshape(-1)

    outgoing = jnp.take(amplitudes, every_cd, axis=1)
    incoming = lax.all_to_all(outgoing, BOTH, split_axis=1, concat_axis=0, tiled=True)
    incoming = incoming.reshape(peer_count, rep_count, rows_own, half_cols)
    integral = lax.dynamic_index_in_dim(integrals, slot, axis=0, keepdims=False)
    integral = integral.reshape(tile_width, rep_count, half_cols)
    halves = jnp.einsum(
        "tric,arc->rtia", incoming, integral, preferred_element_type=jnp.float32
    ).astype(jnp.bfloat16)
    contribution = (halves[0].astype(jnp.float32) + halves[1].astype(jnp.float32)).astype(
        jnp.bfloat16
    ).reshape(peer_count * rows_own, tile_width)

    quarter = local_rows // 2
    lower = contribution[: half_pairs * local_rows].reshape(half_pairs, 2, quarter, tile_width)
    mirrored_rows = jnp.take(contribution, lower_mirror, axis=0).reshape(
        half_pairs, 2, quarter, tile_width
    )
    pairs = jnp.stack([lower, mirrored_rows], axis=2)
    pairs = pairs.transpose(1, 0, 2, 3, 4).reshape(peer_count * rep_count, local_rows, tile_width)
    arrived = lax.all_to_all(pairs, BOTH, split_axis=0, concat_axis=0, tiled=True)

    tile_ids = jnp.arange(residual_in.shape[1], dtype=jnp.int32)
    weights = ((every_ab[:, None] == tile_ids[None, :]) & (every_allowed[:, None] == 1)).astype(
        jnp.bfloat16
    )
    ladder = jnp.einsum("qa,qrc->rac", weights, arrived, preferred_element_type=jnp.float32)
    ladder = ladder.reshape(2, quarter, *ladder.shape[1:])

    to_partner = mirror % local_rows
    inverse = jnp.argsort(to_partner)
    res_a = jnp.where(upper, partner_res[quarter:], residual_in[:quarter])
    res_b = jnp.where(
        upper,
        jnp.take(residual_in, inverse[quarter:], axis=0),
        jnp.take(partner_res, to_partner[:quarter], axis=0),
    )
    summed_a = res_a.astype(jnp.float32) + ladder[0]
    summed_b = res_b.astype(jnp.float32) + ladder[1]
    value = (0.5 * (summed_a - summed_b)).astype(jnp.bfloat16)
    partner_value = partner_2(value, "tile", peer_count.bit_length() - 2)
    by_lower = jnp.where(
        upper,
        jnp.concatenate([partner_value, value]),
        jnp.concatenate([value, partner_value]),
    )
    return jnp.where(upper, -jnp.take(by_lower, to_partner, axis=0), by_lower)


def solution(mesh):
    return jax.shard_map(
        per_device,
        mesh=mesh,
        in_specs=(
            P("tile", None, "rep"),
            P("tile", None, None),
            P("tile"),
            P("tile"),
            P("tile"),
            P(("tile", "rep")),
            P(("tile", "rep"), None, None),
        ),
        out_specs=P(("tile", "rep"), None, None),
        check_vma=False,
    )
```

```python
import jax
import jax.numpy as jnp
from jax import lax
from jax.sharding import PartitionSpec as P

BOTH = ("tile", "rep")


def partner_2(shard, axis, bit):
    return lax.ppermute(shard, axis, [(i, i ^ 1 << bit) for i in range(lax.axis_size(axis))])


def per_device(amplitudes, integrals, task_cd, task_ab, task_allowed, mirror, residual_in):
    peer_count = lax.axis_size("tile")
    rep_count = lax.axis_size("rep")
    rows_own, _, half_cols = amplitudes.shape
    local_rows = residual_in.shape[0]
    tile_width = integrals.shape[1]
    rep = lax.axis_index("rep")

    upper = lax.axis_index("tile") >= peer_count // 2
    partner_res = partner_2(residual_in, "tile", peer_count.bit_length() - 2)

    order = jnp.argsort(1 - task_allowed, stable=True)
    slot = order[rep]
    mine = jnp.concatenate([jnp.stack([task_cd[slot], task_ab[slot], task_allowed[slot]]), mirror])
    mine = jnp.broadcast_to(mine[None], (peer_count * rep_count, mine.shape[0]))
    every = lax.all_to_all(mine, BOTH, split_axis=0, concat_axis=0, tiled=True)
    every_cd, every_ab, every_allowed = every[:, 0], every[:, 1], every[:, 2]

    blocks = rows_own // local_rows
    own_blocks = lax.dynamic_slice_in_dim(every[:, 3:], lax.axis_index("tile") * blocks, blocks)
    inverse_rows = jnp.argsort(own_blocks % local_rows, axis=1)
    inverse_rows = (inverse_rows + local_rows * jnp.arange(blocks)[:, None]).reshape(-1)
    row_order = jnp.where(upper, inverse_rows, jnp.arange(rows_own))

    outgoing = jnp.take(jnp.take(amplitudes, row_order, axis=0), every_cd, axis=1)
    incoming = lax.all_to_all(outgoing, BOTH, split_axis=1, concat_axis=0, tiled=True)
    incoming = incoming.reshape(peer_count, rep_count, rows_own, half_cols)
    integral = lax.dynamic_index_in_dim(integrals, slot, axis=0, keepdims=False)
    integral = integral.reshape(tile_width, rep_count, half_cols)
    halves = jnp.einsum(
        "tric,arc->rtia", incoming, integral, preferred_element_type=jnp.float32
    ).astype(jnp.bfloat16)
    contribution = (halves[0].astype(jnp.float32) + halves[1].astype(jnp.float32)).astype(
        jnp.bfloat16
    )

    quarter = local_rows // 2
    pairs = contribution.reshape(2, peer_count // 2, blocks, 2, quarter, tile_width)
    pairs = pairs.transpose(3, 1, 2, 0, 4, 5).reshape(peer_count * rep_count, local_rows, tile_width)
    arrived = lax.all_to_all(pairs, BOTH, split_axis=0, concat_axis=0, tiled=True)

    tile_ids = jnp.arange(residual_in.shape[1], dtype=jnp.int32)
    weights = ((every_ab[:, None] == tile_ids[None, :]) & (every_allowed[:, None] == 1)).astype(
        jnp.bfloat16
    )
    ladder = jnp.einsum("qa,qrc->rac", weights, arrived, preferred_element_type=jnp.float32)
    ladder = ladder.reshape(2, quarter, *ladder.shape[1:])

    to_partner = mirror % local_rows
    inverse = jnp.argsort(to_partner)
    res_a = jnp.where(upper, partner_res[quarter:], residual_in[:quarter])
    res_b = jnp.where(
        upper,
        jnp.take(residual_in, inverse[quarter:], axis=0),
        jnp.take(partner_res, to_partner[:quarter], axis=0),
    )
    summed_a = res_a.astype(jnp.float32) + ladder[0]
    summed_b = res_b.astype(jnp.float32) + ladder[1]
    value = (0.5 * (summed_a - summed_b)).astype(jnp.bfloat16)
    partner_value = partner_2(value, "tile", peer_count.bit_length() - 2)
    by_lower = jnp.where(
        upper,
        jnp.concatenate([partner_value, value]),
        jnp.concatenate([value, partner_value]),
    )
    return jnp.where(upper, -jnp.take(by_lower, to_partner, axis=0), by_lower)


def solution(mesh):
    return jax.shard_map(
        per_device,
        mesh=mesh,
        in_specs=(
            P("tile", None, "rep"),
            P("tile", None, None),
            P("tile"),
            P("tile"),
            P("tile"),
            P(("tile", "rep")),
            P(("tile", "rep"), None, None),
        ),
        out_specs=P(("tile", "rep"), None, None),
        check_vma=False,
    )
```

```python
import jax
import jax.numpy as jnp
from jax import lax
from jax.sharding import PartitionSpec as P

BOTH = ("tile", "rep")


def partner_2(shard, axis, bit):
    return lax.ppermute(shard, axis, [(i, i ^ 1 << bit) for i in range(lax.axis_size(axis))])


def per_device(amplitudes, integrals, task_cd, task_ab, task_allowed, mirror, residual_in):
    peer_count = lax.axis_size("tile")
    rep_count = lax.axis_size("rep")
    rows_own, _, half_cols = amplitudes.shape
    local_rows = residual_in.shape[0]
    tile_width = integrals.shape[1]
    rep = lax.axis_index("rep")

    upper = lax.axis_index("tile") >= peer_count // 2
    partner_res = partner_2(residual_in, "tile", peer_count.bit_length() - 2)

    order = jnp.argsort(1 - task_allowed, stable=True)
    slot = order[rep]
    mine = jnp.concatenate([jnp.stack([task_cd[slot], task_ab[slot], task_allowed[slot]]), mirror])
    mine = jnp.broadcast_to(mine[None], (peer_count * rep_count, mine.shape[0]))
    every = lax.all_to_all(mine, BOTH, split_axis=0, concat_axis=0, tiled=True)
    every_cd, every_ab, every_allowed = every[:, 0], every[:, 1], every[:, 2]

    blocks = rows_own // local_rows
    own_blocks = lax.dynamic_slice_in_dim(every[:, 3:], lax.axis_index("tile") * blocks, blocks)
    inverse_rows = jnp.argsort(own_blocks % local_rows, axis=1)
    inverse_rows = (inverse_rows + local_rows * jnp.arange(blocks)[:, None]).reshape(-1)
    row_order = jnp.where(upper, inverse_rows, jnp.arange(rows_own))

    outgoing = jnp.take(jnp.take(amplitudes, row_order, axis=0), every_cd, axis=1)
    incoming = lax.all_to_all(outgoing, BOTH, split_axis=1, concat_axis=0, tiled=True)
    incoming = incoming.reshape(peer_count, rep_count, rows_own, half_cols)
    integral = lax.dynamic_index_in_dim(integrals, slot, axis=0, keepdims=False)
    integral = integral.reshape(tile_width, rep_count, half_cols)
    halves = jnp.einsum(
        "tric,arc->rtia", incoming, integral, preferred_element_type=jnp.float32
    ).astype(jnp.bfloat16)
    contribution = (halves[0].astype(jnp.float32) + halves[1].astype(jnp.float32)).astype(
        jnp.bfloat16
    )

    quarter = local_rows // 2
    pairs = contribution.reshape(2, peer_count // 2, blocks, 2, quarter, tile_width)
    pairs = pairs[0].astype(jnp.float32) - pairs[1].astype(jnp.float32)
    pairs = pairs.astype(jnp.bfloat16).transpose(2, 0, 1, 3, 4)
    pairs = pairs.reshape(peer_count * rep_count, quarter, tile_width)
    arrived = lax.all_to_all(pairs, BOTH, split_axis=0, concat_axis=0, tiled=True)

    tile_ids = jnp.arange(residual_in.shape[1], dtype=jnp.int32)
    weights = ((every_ab[:, None] == tile_ids[None, :]) & (every_allowed[:, None] == 1)).astype(
        jnp.bfloat16
    )
    ladder = jnp.einsum("qa,qrc->rac", weights, arrived, preferred_element_type=jnp.float32)

    to_partner = mirror % local_rows
    inverse = jnp.argsort(to_partner)
    res_a = jnp.where(upper, partner_res[quarter:], residual_in[:quarter])
    res_b = jnp.where(
        upper,
        jnp.take(residual_in, inverse[quarter:], axis=0),
        jnp.take(partner_res, to_partner[:quarter], axis=0),
    )
    diff = res_a.astype(jnp.float32) - res_b.astype(jnp.float32)
    value = (0.5 * (diff + ladder)).astype(jnp.bfloat16)
    partner_value = partner_2(value, "tile", peer_count.bit_length() - 2)
    by_lower = jnp.where(
        upper,
        jnp.concatenate([partner_value, value]),
        jnp.concatenate([value, partner_value]),
    )
    return jnp.where(upper, -jnp.take(by_lower, to_partner, axis=0), by_lower)


def solution(mesh):
    return jax.shard_map(
        per_device,
        mesh=mesh,
        in_specs=(
            P("tile", None, "rep"),
            P("tile", None, None),
            P("tile"),
            P("tile"),
            P("tile"),
            P(("tile", "rep")),
            P(("tile", "rep"), None, None),
        ),
        out_specs=P(("tile", "rep"), None, None),
        check_vma=False,
    )
```

```python
import jax
import jax.numpy as jnp
from jax import lax
from jax.sharding import PartitionSpec as P

BOTH = ("tile", "rep")


def partner_2(shard, axis, bit):
    return lax.ppermute(shard, axis, [(i, i ^ 1 << bit) for i in range(lax.axis_size(axis))])


def per_device(amplitudes, integrals, task_cd, task_ab, task_allowed, mirror, residual_in):
    peer_count = lax.axis_size("tile")
    rep_count = lax.axis_size("rep")
    rows_own, _, half_cols = amplitudes.shape
    local_rows = residual_in.shape[0]
    tile_width = integrals.shape[1]
    rep = lax.axis_index("rep")

    upper = lax.axis_index("tile") >= peer_count // 2
    partner_res = partner_2(residual_in, "tile", peer_count.bit_length() - 2)

    order = jnp.argsort(1 - task_allowed, stable=True)
    slot = order[rep]
    mine = jnp.concatenate([jnp.stack([task_cd[slot], task_ab[slot], task_allowed[slot]]), mirror])
    mine = jnp.broadcast_to(mine[None], (peer_count * rep_count, mine.shape[0]))
    every = lax.all_to_all(mine, BOTH, split_axis=0, concat_axis=0, tiled=True)
    every_cd, every_ab, every_allowed = every[:, 0], every[:, 1], every[:, 2]

    blocks = rows_own // local_rows
    own_blocks = lax.dynamic_slice_in_dim(every[:, 3:], lax.axis_index("tile") * blocks, blocks)
    inverse_rows = jnp.argsort(own_blocks % local_rows, axis=1)
    inverse_rows = (inverse_rows + local_rows * jnp.arange(blocks)[:, None]).reshape(-1)
    row_order = jnp.where(upper, inverse_rows, jnp.arange(rows_own))

    outgoing = jnp.take(jnp.take(amplitudes, row_order, axis=0), every_cd, axis=1)
    incoming = lax.all_to_all(outgoing, BOTH, split_axis=1, concat_axis=0, tiled=True)
    incoming = incoming.reshape(peer_count, rep_count, rows_own, half_cols)
    partner_res, incoming = lax.optimization_barrier((partner_res, incoming))
    integral = lax.dynamic_index_in_dim(integrals, slot, axis=0, keepdims=False)
    integral = integral.reshape(tile_width, rep_count, half_cols)
    halves = jnp.einsum(
        "tric,arc->rtia", incoming, integral, preferred_element_type=jnp.float32
    ).astype(jnp.bfloat16)
    contribution = (halves[0].astype(jnp.float32) + halves[1].astype(jnp.float32)).astype(
        jnp.bfloat16
    )

    quarter = local_rows // 2
    pairs = contribution.reshape(2, peer_count // 2, blocks, 2, quarter, tile_width)
    pairs = pairs[0].astype(jnp.float32) - pairs[1].astype(jnp.float32)
    pairs = pairs.astype(jnp.bfloat16).transpose(2, 0, 1, 3, 4)
    pairs = pairs.reshape(peer_count * rep_count, quarter, tile_width)
    arrived = lax.all_to_all(pairs, BOTH, split_axis=0, concat_axis=0, tiled=True)

    tile_ids = jnp.arange(residual_in.shape[1], dtype=jnp.int32)
    weights = ((every_ab[:, None] == tile_ids[None, :]) & (every_allowed[:, None] == 1)).astype(
        jnp.bfloat16
    )
    ladder = jnp.einsum("qa,qrc->rac", weights, arrived, preferred_element_type=jnp.float32)

    to_partner = mirror % local_rows
    inverse = jnp.argsort(to_partner)
    res_a = jnp.where(upper, partner_res[quarter:], residual_in[:quarter])
    res_b = jnp.where(
        upper,
        jnp.take(residual_in, inverse[quarter:], axis=0),
        jnp.take(partner_res, to_partner[:quarter], axis=0),
    )
    diff = res_a.astype(jnp.float32) - res_b.astype(jnp.float32)
    value = (0.5 * (diff + ladder)).astype(jnp.bfloat16)
    partner_value = partner_2(value, "tile", peer_count.bit_length() - 2)
    by_lower = jnp.where(
        upper,
        jnp.concatenate([partner_value, value]),
        jnp.concatenate([value, partner_value]),
    )
    return jnp.where(upper, -jnp.take(by_lower, to_partner, axis=0), by_lower)


def solution(mesh):
    return jax.shard_map(
        per_device,
        mesh=mesh,
        in_specs=(
            P("tile", None, "rep"),
            P("tile", None, None),
            P("tile"),
            P("tile"),
            P("tile"),
            P(("tile", "rep")),
            P(("tile", "rep"), None, None),
        ),
        out_specs=P(("tile", "rep"), None, None),
        check_vma=False,
    )
```

```python
import jax
import jax.numpy as jnp
from jax import lax
from jax.sharding import PartitionSpec as P

BOTH = ("tile", "rep")


def partner_2(shard, axis, bit):
    return lax.ppermute(shard, axis, [(i, i ^ 1 << bit) for i in range(lax.axis_size(axis))])


def per_device(amplitudes, integrals, task_cd, task_ab, task_allowed, mirror, residual_in):
    peer_count = lax.axis_size("tile")
    rep_count = lax.axis_size("rep")
    rows_own, _, half_cols = amplitudes.shape
    local_rows = residual_in.shape[0]
    tile_width = integrals.shape[1]
    rep = lax.axis_index("rep")

    upper = lax.axis_index("tile") >= peer_count // 2
    partner_res = partner_2(residual_in, "tile", peer_count.bit_length() - 2)

    allowed = task_allowed == 1
    first = jnp.where(allowed[0], 0, jnp.where(allowed[1], 1, 2))
    second = jnp.where(
        allowed[2] & (first < 2), 2, jnp.where(allowed[1] & (first < 1), 1, (first + 1) % 3)
    )
    slot = jnp.where(rep == 0, first, second)
    pick = jnp.arange(task_cd.shape[0]) == slot
    chosen = [jnp.sum(jnp.where(pick, ids, 0)) for ids in (task_cd, task_ab, task_allowed)]
    mine = jnp.concatenate([jnp.stack(chosen), mirror])
    mine = jnp.broadcast_to(mine[None], (peer_count * rep_count, mine.shape[0]))
    every = lax.all_to_all(mine, BOTH, split_axis=0, concat_axis=0, tiled=True)
    every_cd, every_ab, every_allowed = every[:, 0], every[:, 1], every[:, 2]

    blocks = rows_own // local_rows
    own_blocks = lax.dynamic_slice_in_dim(every[:, 3:], lax.axis_index("tile") * blocks, blocks)
    inverse_rows = jnp.argsort(own_blocks % local_rows, axis=1)
    inverse_rows = (inverse_rows + local_rows * jnp.arange(blocks)[:, None]).reshape(-1)
    row_order = jnp.where(upper, inverse_rows, jnp.arange(rows_own))

    by_cd = jnp.take(amplitudes.transpose(1, 0, 2), row_order, axis=1)
    outgoing = jnp.take(by_cd, every_cd, axis=0)
    incoming = lax.all_to_all(outgoing, BOTH, split_axis=0, concat_axis=0, tiled=True)
    incoming = incoming.reshape(peer_count, rep_count, rows_own, half_cols)
    partner_res, incoming = lax.optimization_barrier((partner_res, incoming))
    integral = lax.dynamic_index_in_dim(integrals, slot, axis=0, keepdims=False)
    integral = integral.reshape(tile_width, rep_count, half_cols)
    halves = jnp.einsum(
        "tric,arc->rtia", incoming, integral, preferred_element_type=jnp.float32
    ).astype(jnp.bfloat16)
    contribution = (halves[0].astype(jnp.float32) + halves[1].astype(jnp.float32)).astype(
        jnp.bfloat16
    )

    quarter = local_rows // 2
    pairs = contribution.reshape(2, peer_count // 2, blocks, 2, quarter, tile_width)
    pairs = pairs[0].astype(jnp.float32) - pairs[1].astype(jnp.float32)
    pairs = pairs.astype(jnp.bfloat16).transpose(2, 0, 1, 3, 4)
    pairs = pairs.reshape(peer_count * rep_count, quarter, tile_width)
    arrived = lax.all_to_all(pairs, BOTH, split_axis=0, concat_axis=0, tiled=True)

    tile_ids = jnp.arange(residual_in.shape[1], dtype=jnp.int32)
    weights = ((every_ab[:, None] == tile_ids[None, :]) & (every_allowed[:, None] == 1)).astype(
        jnp.bfloat16
    )
    ladder = jnp.einsum("qa,qrc->rac", weights, arrived, preferred_element_type=jnp.float32)

    to_partner = mirror % local_rows
    inverse = jnp.argsort(to_partner)
    res_a = jnp.where(upper, partner_res[quarter:], residual_in[:quarter])
    res_b = jnp.where(
        upper,
        jnp.take(residual_in, inverse[quarter:], axis=0),
        jnp.take(partner_res, to_partner[:quarter], axis=0),
    )
    diff = res_a.astype(jnp.float32) - res_b.astype(jnp.float32)
    value = (0.5 * (diff + ladder)).astype(jnp.bfloat16)
    partner_value = partner_2(value, "tile", peer_count.bit_length() - 2)
    by_lower = jnp.where(
        upper,
        jnp.concatenate([partner_value, value]),
        jnp.concatenate([value, partner_value]),
    )
    return jnp.where(upper, -jnp.take(by_lower, to_partner, axis=0), by_lower)


def solution(mesh):
    return jax.shard_map(
        per_device,
        mesh=mesh,
        in_specs=(
            P("tile", None, "rep"),
            P("tile", None, None),
            P("tile"),
            P("tile"),
            P("tile"),
            P(("tile", "rep")),
            P(("tile", "rep"), None, None),
        ),
        out_specs=P(("tile", "rep"), None, None),
        check_vma=False,
    )
```

```python
import jax
import jax.numpy as jnp
from jax import lax
from jax.sharding import PartitionSpec as P

BOTH = ("tile", "rep")


def partner_2(shard, axis, bit):
    return lax.ppermute(shard, axis, [(i, i ^ 1 << bit) for i in range(lax.axis_size(axis))])


def per_device(amplitudes, integrals, task_cd, task_ab, task_allowed, mirror, residual_in):
    peer_count = lax.axis_size("tile")
    rep_count = lax.axis_size("rep")
    rows_own, _, half_cols = amplitudes.shape
    local_rows = residual_in.shape[0]
    tile_width = integrals.shape[1]
    rep = lax.axis_index("rep")

    upper = lax.axis_index("tile") >= peer_count // 2
    partner_res = partner_2(residual_in, "tile", peer_count.bit_length() - 2)

    allowed = task_allowed == 1
    first = jnp.where(allowed[0], 0, jnp.where(allowed[1], 1, 2))
    second = jnp.where(
        allowed[2] & (first < 2), 2, jnp.where(allowed[1] & (first < 1), 1, (first + 1) % 3)
    )
    slot = jnp.where(rep == 0, first, second)
    pick = jnp.arange(task_cd.shape[0]) == slot
    chosen = [jnp.sum(jnp.where(pick, ids, 0)) for ids in (task_cd, task_ab, task_allowed)]
    mine = jnp.concatenate([jnp.stack(chosen), mirror])
    mine = jnp.broadcast_to(mine[None], (peer_count * rep_count, mine.shape[0]))
    every = lax.all_to_all(mine, BOTH, split_axis=0, concat_axis=0, tiled=True)
    every_cd, every_ab, every_allowed = every[:, 0], every[:, 1], every[:, 2]

    blocks = rows_own // local_rows
    own_blocks = lax.dynamic_slice_in_dim(every[:, 3:], lax.axis_index("tile") * blocks, blocks)
    inverse_rows = jnp.argsort(own_blocks % local_rows, axis=1)
    inverse_rows = (inverse_rows + local_rows * jnp.arange(blocks)[:, None]).reshape(-1)
    row_order = jnp.where(upper, inverse_rows, jnp.arange(rows_own))

    by_cd = jnp.take(amplitudes.transpose(1, 0, 2), row_order, axis=1, mode="clip")
    outgoing = jnp.take(by_cd, every_cd, axis=0, mode="clip")
    incoming = lax.all_to_all(outgoing, BOTH, split_axis=0, concat_axis=0, tiled=True)
    incoming = incoming.reshape(peer_count, rep_count, rows_own, half_cols)
    partner_res, incoming = lax.optimization_barrier((partner_res, incoming))
    integral = lax.dynamic_index_in_dim(integrals, slot, axis=0, keepdims=False)
    integral = integral.reshape(tile_width, rep_count, half_cols)
    halves = jnp.einsum(
        "tric,arc->rtia", incoming, integral, preferred_element_type=jnp.float32
    ).astype(jnp.bfloat16)
    contribution = (halves[0].astype(jnp.float32) + halves[1].astype(jnp.float32)).astype(
        jnp.bfloat16
    )

    quarter = local_rows // 2
    pairs = contribution.reshape(2, peer_count // 2, blocks, 2, quarter, tile_width)
    pairs = pairs[0].astype(jnp.float32) - pairs[1].astype(jnp.float32)
    pairs = pairs.astype(jnp.bfloat16).transpose(2, 0, 1, 3, 4)
    pairs = pairs.reshape(peer_count * rep_count, quarter, tile_width)
    arrived = lax.all_to_all(pairs, BOTH, split_axis=0, concat_axis=0, tiled=True)

    tile_ids = jnp.arange(residual_in.shape[1], dtype=jnp.int32)
    weights = ((every_ab[:, None] == tile_ids[None, :]) & (every_allowed[:, None] == 1)).astype(
        jnp.bfloat16
    )
    ladder = jnp.einsum("qa,qrc->rac", weights, arrived, preferred_element_type=jnp.float32)

    to_partner = mirror % local_rows
    inverse = jnp.argsort(to_partner)
    res_a = jnp.where(upper, partner_res[quarter:], residual_in[:quarter])
    res_b = jnp.where(
        upper,
        jnp.take(residual_in, inverse[quarter:], axis=0, mode="clip"),
        jnp.take(partner_res, to_partner[:quarter], axis=0, mode="clip"),
    )
    diff = res_a.astype(jnp.float32) - res_b.astype(jnp.float32)
    value = (0.5 * (diff + ladder)).astype(jnp.bfloat16)
    partner_value = partner_2(value, "tile", peer_count.bit_length() - 2)
    by_lower = jnp.where(
        upper,
        jnp.concatenate([partner_value, value]),
        jnp.concatenate([value, partner_value]),
    )
    return jnp.where(upper, -jnp.take(by_lower, to_partner, axis=0, mode="clip"), by_lower)


def solution(mesh):
    return jax.shard_map(
        per_device,
        mesh=mesh,
        in_specs=(
            P("tile", None, "rep"),
            P("tile", None, None),
            P("tile"),
            P("tile"),
            P("tile"),
            P(("tile", "rep")),
            P(("tile", "rep"), None, None),
        ),
        out_specs=P(("tile", "rep"), None, None),
        check_vma=False,
    )
```

```python
import jax
import jax.numpy as jnp
from jax import lax
from jax.sharding import PartitionSpec as P

BOTH = ("tile", "rep")


def partner_2(shard, axis, bit):
    return lax.ppermute(shard, axis, [(i, i ^ 1 << bit) for i in range(lax.axis_size(axis))])


def per_device(amplitudes, integrals, task_cd, task_ab, task_allowed, mirror, residual_in):
    peer_count = lax.axis_size("tile")
    rep_count = lax.axis_size("rep")
    rows_own, _, half_cols = amplitudes.shape
    local_rows = residual_in.shape[0]
    tile_width = integrals.shape[1]
    rep = lax.axis_index("rep")

    upper = lax.axis_index("tile") >= peer_count // 2
    partner_res = partner_2(residual_in, "tile", peer_count.bit_length() - 2)

    allowed = task_allowed == 1
    first = jnp.where(allowed[0], 0, jnp.where(allowed[1], 1, 2))
    second = jnp.where(
        allowed[2] & (first < 2), 2, jnp.where(allowed[1] & (first < 1), 1, (first + 1) % 3)
    )
    slot = jnp.where(rep == 0, first, second)
    pick = jnp.arange(task_cd.shape[0]) == slot
    chosen = [jnp.sum(jnp.where(pick, ids, 0)) for ids in (task_cd, task_ab, task_allowed)]
    mine = jnp.concatenate([jnp.stack(chosen), mirror])
    mine = jnp.broadcast_to(mine[None], (peer_count * rep_count, mine.shape[0]))
    every = lax.all_to_all(mine, BOTH, split_axis=0, concat_axis=0, tiled=True)
    every_cd, every_ab, every_allowed = every[:, 0], every[:, 1], every[:, 2]

    blocks = rows_own // local_rows
    own_blocks = lax.dynamic_slice_in_dim(every[:, 3:], lax.axis_index("tile") * blocks, blocks)
    inverse_rows = jnp.argsort(own_blocks % local_rows, axis=1)
    inverse_rows = (inverse_rows + local_rows * jnp.arange(blocks)[:, None]).reshape(-1)
    row_order = jnp.where(upper, inverse_rows, jnp.arange(rows_own))

    outgoing = amplitudes.at[row_order[None, :], every_cd[:, None]].get(mode="clip")
    incoming = lax.all_to_all(outgoing, BOTH, split_axis=0, concat_axis=0, tiled=True)
    incoming = incoming.reshape(peer_count, rep_count, rows_own, half_cols)
    partner_res, incoming = lax.optimization_barrier((partner_res, incoming))
    integral = lax.dynamic_index_in_dim(integrals, slot, axis=0, keepdims=False)
    integral = integral.reshape(tile_width, rep_count, half_cols)
    halves = jnp.einsum(
        "tric,arc->rtia", incoming, integral, preferred_element_type=jnp.float32
    ).astype(jnp.bfloat16)
    contribution = (halves[0].astype(jnp.float32) + halves[1].astype(jnp.float32)).astype(
        jnp.bfloat16
    )

    quarter = local_rows // 2
    pairs = contribution.reshape(2, peer_count // 2, blocks, 2, quarter, tile_width)
    pairs = pairs[0].astype(jnp.float32) - pairs[1].astype(jnp.float32)
    pairs = pairs.astype(jnp.bfloat16).transpose(2, 0, 1, 3, 4)
    pairs = pairs.reshape(peer_count * rep_count, quarter, tile_width)
    arrived = lax.all_to_all(pairs, BOTH, split_axis=0, concat_axis=0, tiled=True)

    tile_ids = jnp.arange(residual_in.shape[1], dtype=jnp.int32)
    weights = ((every_ab[:, None] == tile_ids[None, :]) & (every_allowed[:, None] == 1)).astype(
        jnp.bfloat16
    )
    ladder = jnp.einsum("qa,qrc->rac", weights, arrived, preferred_element_type=jnp.float32)

    to_partner = mirror % local_rows
    inverse = jnp.argsort(to_partner)
    res_a = jnp.where(upper, partner_res[quarter:], residual_in[:quarter])
    res_b = jnp.where(
        upper,
        jnp.take(residual_in, inverse[quarter:], axis=0, mode="clip"),
        jnp.take(partner_res, to_partner[:quarter], axis=0, mode="clip"),
    )
    diff = res_a.astype(jnp.float32) - res_b.astype(jnp.float32)
    value = (0.5 * (diff + ladder)).astype(jnp.bfloat16)
    partner_value = partner_2(value, "tile", peer_count.bit_length() - 2)
    by_lower = jnp.concatenate(
        [jnp.where(upper, partner_value, value), jnp.where(upper, value, partner_value)]
    )
    place = jnp.where(upper, to_partner, jnp.arange(local_rows))
    sign = jnp.where(upper, -1.0, 1.0).astype(jnp.bfloat16)
    return sign * jnp.take(by_lower, place, axis=0, mode="clip")


def solution(mesh):
    return jax.shard_map(
        per_device,
        mesh=mesh,
        in_specs=(
            P("tile", None, "rep"),
            P("tile", None, None),
            P("tile"),
            P("tile"),
            P("tile"),
            P(("tile", "rep")),
            P(("tile", "rep"), None, None),
        ),
        out_specs=P(("tile", "rep"), None, None),
        check_vma=False,
    )
```

```python
import jax
import jax.numpy as jnp
from jax import lax
from jax.sharding import PartitionSpec as P

BOTH = ("tile", "rep")


def partner_2(shard, axis, bit):
    return lax.ppermute(shard, axis, [(i, i ^ 1 << bit) for i in range(lax.axis_size(axis))])


def per_device(amplitudes, integrals, task_cd, task_ab, task_allowed, mirror, residual_in):
    peer_count = lax.axis_size("tile")
    rep_count = lax.axis_size("rep")
    rows_own, _, half_cols = amplitudes.shape
    local_rows = residual_in.shape[0]
    tile_width = integrals.shape[1]
    rep = lax.axis_index("rep")

    upper = lax.axis_index("tile") >= peer_count // 2
    partner_res = partner_2(residual_in, "tile", peer_count.bit_length() - 2)

    allowed = task_allowed == 1
    first = jnp.where(allowed[0], 0, jnp.where(allowed[1], 1, 2))
    second = jnp.where(
        allowed[2] & (first < 2), 2, jnp.where(allowed[1] & (first < 1), 1, (first + 1) % 3)
    )
    slot = jnp.where(rep == 0, first, second)
    pick = jnp.arange(task_cd.shape[0]) == slot
    chosen = [jnp.sum(jnp.where(pick, ids, 0)) for ids in (task_cd, task_ab, task_allowed)]
    mine = jnp.concatenate([jnp.stack(chosen), mirror])
    mine = jnp.broadcast_to(mine[None], (peer_count * rep_count, mine.shape[0]))
    every = lax.all_to_all(mine, BOTH, split_axis=0, concat_axis=0, tiled=True)
    every_cd, every_ab, every_allowed = every[:, 0], every[:, 1], every[:, 2]

    blocks = rows_own // local_rows
    own_blocks = lax.dynamic_slice_in_dim(every[:, 3:], lax.axis_index("tile") * blocks, blocks)
    inverse_rows = jnp.argsort(own_blocks % local_rows, axis=1)
    inverse_rows = (inverse_rows + local_rows * jnp.arange(blocks)[:, None]).reshape(-1)
    row_order = jnp.where(upper, inverse_rows, jnp.arange(rows_own))

    by_row = jnp.take(amplitudes, row_order, axis=0, mode="clip")
    outgoing = jnp.take(by_row, every_cd, axis=1, mode="clip")
    incoming = lax.all_to_all(outgoing, BOTH, split_axis=1, concat_axis=0, tiled=True)
    incoming = incoming.reshape(peer_count, rep_count, rows_own, half_cols)
    partner_res, incoming = lax.optimization_barrier((partner_res, incoming))
    integral = lax.dynamic_index_in_dim(integrals, slot, axis=0, keepdims=False)
    integral = integral.reshape(tile_width, rep_count, half_cols)
    halves = jnp.einsum(
        "tric,arc->rtia", incoming, integral, preferred_element_type=jnp.float32
    ).astype(jnp.bfloat16)
    contribution = (halves[0].astype(jnp.float32) + halves[1].astype(jnp.float32)).astype(
        jnp.bfloat16
    )

    quarter = local_rows // 2
    pairs = contribution.reshape(2, peer_count // 2, blocks, 2, quarter, tile_width)
    pairs = pairs[0].astype(jnp.float32) - pairs[1].astype(jnp.float32)
    pairs = pairs.astype(jnp.bfloat16).transpose(2, 0, 1, 3, 4)
    pairs = pairs.reshape(peer_count * rep_count, quarter, tile_width)
    arrived = lax.all_to_all(pairs, BOTH, split_axis=0, concat_axis=0, tiled=True)

    tile_ids = jnp.arange(residual_in.shape[1], dtype=jnp.int32)
    weights = ((every_ab[:, None] == tile_ids[None, :]) & (every_allowed[:, None] == 1)).astype(
        jnp.bfloat16
    )
    ladder = jnp.einsum("qa,qrc->rac", weights, arrived, preferred_element_type=jnp.float32)

    to_partner = mirror % local_rows
    inverse = jnp.argsort(to_partner)
    res_a = jnp.where(upper, partner_res[quarter:], residual_in[:quarter])
    res_b = jnp.where(
        upper,
        jnp.take(residual_in, inverse[quarter:], axis=0, mode="clip"),
        jnp.take(partner_res, to_partner[:quarter], axis=0, mode="clip"),
    )
    diff = res_a.astype(jnp.float32) - res_b.astype(jnp.float32)
    value = (0.5 * (diff + ladder)).astype(jnp.bfloat16)
    partner_value = partner_2(value, "tile", peer_count.bit_length() - 2)
    by_lower = jnp.concatenate(
        [jnp.where(upper, partner_value, value), jnp.where(upper, value, partner_value)]
    )
    place = jnp.where(upper, to_partner, jnp.arange(local_rows))
    sign = jnp.where(upper, -1.0, 1.0).astype(jnp.bfloat16)
    return sign * jnp.take(by_lower, place, axis=0, mode="clip")


def solution(mesh):
    return jax.shard_map(
        per_device,
        mesh=mesh,
        in_specs=(
            P("tile", None, "rep"),
            P("tile", None, None),
            P("tile"),
            P("tile"),
            P("tile"),
            P(("tile", "rep")),
            P(("tile", "rep"), None, None),
        ),
        out_specs=P(("tile", "rep"), None, None),
        check_vma=False,
    )
```

```python
import jax
import jax.numpy as jnp
from jax import lax
from jax.sharding import PartitionSpec as P

BOTH = ("tile", "rep")


def partner_2(shard, axis, bit):
    return lax.ppermute(shard, axis, [(i, i ^ 1 << bit) for i in range(lax.axis_size(axis))])


def per_device(amplitudes, integrals, task_cd, task_ab, task_allowed, mirror, residual_in):
    peer_count = lax.axis_size("tile")
    rep_count = lax.axis_size("rep")
    rows_own, _, half_cols = amplitudes.shape
    local_rows = residual_in.shape[0]
    tile_width = integrals.shape[1]
    rep = lax.axis_index("rep")

    upper = lax.axis_index("tile") >= peer_count // 2
    partner_res = partner_2(residual_in, "tile", peer_count.bit_length() - 2)

    allowed = task_allowed == 1
    first = jnp.where(allowed[0], 0, jnp.where(allowed[1], 1, 2))
    second = jnp.where(
        allowed[2] & (first < 2), 2, jnp.where(allowed[1] & (first < 1), 1, (first + 1) % 3)
    )
    slot = jnp.where(rep == 0, first, second)
    pick = jnp.arange(task_cd.shape[0]) == slot
    chosen = [jnp.sum(jnp.where(pick, ids, 0)) for ids in (task_cd, task_ab, task_allowed)]
    mine = jnp.concatenate([jnp.stack(chosen), mirror])
    mine = jnp.broadcast_to(mine[None], (peer_count * rep_count, mine.shape[0]))
    every = lax.all_to_all(mine, BOTH, split_axis=0, concat_axis=0, tiled=True)
    every_cd, every_ab, every_allowed = every[:, 0], every[:, 1], every[:, 2]

    blocks = rows_own // local_rows
    own_blocks = lax.dynamic_slice_in_dim(every[:, 3:], lax.axis_index("tile") * blocks, blocks)
    inverse_rows = jnp.argsort(own_blocks % local_rows, axis=1)
    inverse_rows = (inverse_rows + local_rows * jnp.arange(blocks)[:, None]).reshape(-1)
    row_order = jnp.where(upper, inverse_rows, jnp.arange(rows_own))

    reorder = (row_order[:, None] == jnp.arange(rows_own)[None, :]).astype(amplitudes.dtype)
    by_row = jnp.einsum(
        "ij,jdc->idc", reorder, amplitudes, preferred_element_type=jnp.float32
    ).astype(amplitudes.dtype)
    outgoing = jnp.take(by_row, every_cd, axis=1, mode="clip")
    incoming = lax.all_to_all(outgoing, BOTH, split_axis=1, concat_axis=0, tiled=True)
    incoming = incoming.reshape(peer_count, rep_count, rows_own, half_cols)
    partner_res, incoming = lax.optimization_barrier((partner_res, incoming))
    integral = lax.dynamic_index_in_dim(integrals, slot, axis=0, keepdims=False)
    integral = integral.reshape(tile_width, rep_count, half_cols)
    halves = jnp.einsum(
        "tric,arc->rtia", incoming, integral, preferred_element_type=jnp.float32
    ).astype(jnp.bfloat16)
    contribution = (halves[0].astype(jnp.float32) + halves[1].astype(jnp.float32)).astype(
        jnp.bfloat16
    )

    quarter = local_rows // 2
    pairs = contribution.reshape(2, peer_count // 2, blocks, 2, quarter, tile_width)
    pairs = pairs[0].astype(jnp.float32) - pairs[1].astype(jnp.float32)
    pairs = pairs.astype(jnp.bfloat16).transpose(2, 0, 1, 3, 4)
    pairs = pairs.reshape(peer_count * rep_count, quarter, tile_width)
    arrived = lax.all_to_all(pairs, BOTH, split_axis=0, concat_axis=0, tiled=True)

    tile_ids = jnp.arange(residual_in.shape[1], dtype=jnp.int32)
    weights = ((every_ab[:, None] == tile_ids[None, :]) & (every_allowed[:, None] == 1)).astype(
        jnp.bfloat16
    )
    ladder = jnp.einsum("qa,qrc->rac", weights, arrived, preferred_element_type=jnp.float32)

    to_partner = mirror % local_rows
    inverse = jnp.argsort(to_partner)
    res_a = jnp.where(upper, partner_res[quarter:], residual_in[:quarter])
    res_b = jnp.where(
        upper,
        jnp.take(residual_in, inverse[quarter:], axis=0, mode="clip"),
        jnp.take(partner_res, to_partner[:quarter], axis=0, mode="clip"),
    )
    diff = res_a.astype(jnp.float32) - res_b.astype(jnp.float32)
    value = (0.5 * (diff + ladder)).astype(jnp.bfloat16)
    partner_value = partner_2(value, "tile", peer_count.bit_length() - 2)
    by_lower = jnp.concatenate(
        [jnp.where(upper, partner_value, value), jnp.where(upper, value, partner_value)]
    )
    place = jnp.where(upper, to_partner, jnp.arange(local_rows))
    sign = jnp.where(upper, -1.0, 1.0).astype(jnp.bfloat16)
    return sign * jnp.take(by_lower, place, axis=0, mode="clip")


def solution(mesh):
    return jax.shard_map(
        per_device,
        mesh=mesh,
        in_specs=(
            P("tile", None, "rep"),
            P("tile", None, None),
            P("tile"),
            P("tile"),
            P("tile"),
            P(("tile", "rep")),
            P(("tile", "rep"), None, None),
        ),
        out_specs=P(("tile", "rep"), None, None),
        check_vma=False,
    )
```

```python
import jax
import jax.numpy as jnp
from jax import lax
from jax.sharding import PartitionSpec as P

BOTH = ("tile", "rep")


def partner_2(shard, axis, bit):
    return lax.ppermute(shard, axis, [(i, i ^ 1 << bit) for i in range(lax.axis_size(axis))])


def per_device(amplitudes, integrals, task_cd, task_ab, task_allowed, mirror, residual_in):
    peer_count = lax.axis_size("tile")
    rep_count = lax.axis_size("rep")
    rows_own, _, half_cols = amplitudes.shape
    local_rows = residual_in.shape[0]
    tile_width = integrals.shape[1]
    rep = lax.axis_index("rep")

    upper = lax.axis_index("tile") >= peer_count // 2
    partner_res = partner_2(residual_in, "tile", peer_count.bit_length() - 2)

    allowed = task_allowed == 1
    first = jnp.where(allowed[0], 0, jnp.where(allowed[1], 1, 2))
    second = jnp.where(
        allowed[2] & (first < 2), 2, jnp.where(allowed[1] & (first < 1), 1, (first + 1) % 3)
    )
    slot = jnp.where(rep == 0, first, second)
    pick = jnp.arange(task_cd.shape[0]) == slot
    chosen = [jnp.sum(jnp.where(pick, ids, 0)) for ids in (task_cd, task_ab, task_allowed)]
    pair_span = 2 * peer_count * rep_count * local_rows
    code = chosen[0] + 256 * (chosen[1] + 256 * chosen[2])
    mine = jnp.broadcast_to((mirror + pair_span * code)[None], (peer_count * rep_count, local_rows))
    every = lax.all_to_all(mine, BOTH, split_axis=0, concat_axis=0, tiled=True)
    packed = every[:, 0] // pair_span
    every_cd, every_ab, every_allowed = packed % 256, packed // 256 % 256, packed // 65536
    every = jnp.concatenate([jnp.zeros((every.shape[0], 3), every.dtype), every % pair_span], axis=1)

    blocks = rows_own // local_rows
    own_blocks = lax.dynamic_slice_in_dim(every[:, 3:], lax.axis_index("tile") * blocks, blocks)
    inverse_rows = jnp.argsort(own_blocks % local_rows, axis=1)
    inverse_rows = (inverse_rows + local_rows * jnp.arange(blocks)[:, None]).reshape(-1)
    row_order = jnp.where(upper, inverse_rows, jnp.arange(rows_own))

    reorder = (row_order[:, None] == jnp.arange(rows_own)[None, :]).astype(amplitudes.dtype)
    by_row = jnp.einsum(
        "ij,jdc->idc", reorder, amplitudes, preferred_element_type=jnp.float32
    ).astype(amplitudes.dtype)
    outgoing = jnp.take(by_row, every_cd, axis=1, mode="clip")
    incoming = lax.all_to_all(outgoing, BOTH, split_axis=1, concat_axis=0, tiled=True)
    incoming = incoming.reshape(peer_count, rep_count, rows_own, half_cols)
    partner_res, incoming = lax.optimization_barrier((partner_res, incoming))
    integral = lax.dynamic_index_in_dim(integrals, slot, axis=0, keepdims=False)
    integral = integral.reshape(tile_width, rep_count, half_cols)
    halves = jnp.einsum(
        "tric,arc->rtia", incoming, integral, preferred_element_type=jnp.float32
    ).astype(jnp.bfloat16)
    contribution = (halves[0].astype(jnp.float32) + halves[1].astype(jnp.float32)).astype(
        jnp.bfloat16
    )

    quarter = local_rows // 2
    pairs = contribution.reshape(2, peer_count // 2, blocks, 2, quarter, tile_width)
    pairs = pairs[0].astype(jnp.float32) - pairs[1].astype(jnp.float32)
    pairs = pairs.astype(jnp.bfloat16).transpose(2, 0, 1, 3, 4)
    pairs = pairs.reshape(peer_count * rep_count, quarter, tile_width)
    arrived = lax.all_to_all(pairs, BOTH, split_axis=0, concat_axis=0, tiled=True)

    tile_ids = jnp.arange(residual_in.shape[1], dtype=jnp.int32)
    weights = ((every_ab[:, None] == tile_ids[None, :]) & (every_allowed[:, None] == 1)).astype(
        jnp.bfloat16
    )
    ladder = jnp.einsum("qa,qrc->rac", weights, arrived, preferred_element_type=jnp.float32)

    to_partner = mirror % local_rows
    inverse = jnp.argsort(to_partner)
    res_a = jnp.where(upper, partner_res[quarter:], residual_in[:quarter])
    res_b = jnp.where(
        upper,
        jnp.take(residual_in, inverse[quarter:], axis=0, mode="clip"),
        jnp.take(partner_res, to_partner[:quarter], axis=0, mode="clip"),
    )
    diff = res_a.astype(jnp.float32) - res_b.astype(jnp.float32)
    value = (0.5 * (diff + ladder)).astype(jnp.bfloat16)
    partner_value = partner_2(value, "tile", peer_count.bit_length() - 2)
    by_lower = jnp.concatenate(
        [jnp.where(upper, partner_value, value), jnp.where(upper, value, partner_value)]
    )
    place = jnp.where(upper, to_partner, jnp.arange(local_rows))
    sign = jnp.where(upper, -1.0, 1.0).astype(jnp.bfloat16)
    return sign * jnp.take(by_lower, place, axis=0, mode="clip")


def solution(mesh):
    return jax.shard_map(
        per_device,
        mesh=mesh,
        in_specs=(
            P("tile", None, "rep"),
            P("tile", None, None),
            P("tile"),
            P("tile"),
            P("tile"),
            P(("tile", "rep")),
            P(("tile", "rep"), None, None),
        ),
        out_specs=P(("tile", "rep"), None, None),
        check_vma=False,
    )
```

```python
import jax
import jax.numpy as jnp
from jax import lax
from jax.sharding import PartitionSpec as P

BOTH = ("tile", "rep")


def partner_2(shard, axis, bit):
    return lax.ppermute(shard, axis, [(i, i ^ 1 << bit) for i in range(lax.axis_size(axis))])


def per_device(amplitudes, integrals, task_cd, task_ab, task_allowed, mirror, residual_in):
    peer_count = lax.axis_size("tile")
    rep_count = lax.axis_size("rep")
    rows_own, _, half_cols = amplitudes.shape
    local_rows = residual_in.shape[0]
    tile_width = integrals.shape[1]
    rep = lax.axis_index("rep")

    upper = lax.axis_index("tile") >= peer_count // 2
    partner_res = partner_2(residual_in, "tile", peer_count.bit_length() - 2)

    allowed = task_allowed == 1
    first = jnp.where(allowed[0], 0, jnp.where(allowed[1], 1, 2))
    second = jnp.where(
        allowed[2] & (first < 2), 2, jnp.where(allowed[1] & (first < 1), 1, (first + 1) % 3)
    )
    slot = jnp.where(rep == 0, first, second)
    pick = jnp.arange(task_cd.shape[0]) == slot
    chosen = [jnp.sum(jnp.where(pick, ids, 0)) for ids in (task_cd, task_ab, task_allowed)]
    mine = jnp.concatenate([jnp.stack(chosen), mirror])
    mine = jnp.broadcast_to(mine[None], (peer_count * rep_count, mine.shape[0]))
    every = lax.all_to_all(mine, BOTH, split_axis=0, concat_axis=0, tiled=True)
    every_cd, every_ab, every_allowed = every[:, 0], every[:, 1], every[:, 2]

    blocks = rows_own // local_rows
    own_blocks = lax.dynamic_slice_in_dim(every[:, 3:], lax.axis_index("tile") * blocks, blocks)
    inverse_rows = jnp.argsort(own_blocks % local_rows, axis=1)
    inverse_rows = (inverse_rows + local_rows * jnp.arange(blocks)[:, None]).reshape(-1)
    row_order = jnp.where(upper, inverse_rows, jnp.arange(rows_own))

    reorder = (row_order[:, None] == jnp.arange(rows_own)[None, :]).astype(amplitudes.dtype)
    by_row = jnp.einsum(
        "ij,jdc->idc", reorder, amplitudes, preferred_element_type=jnp.float32
    ).astype(amplitudes.dtype)
    outgoing = jnp.take(by_row, every_cd, axis=1, mode="clip")
    incoming = lax.all_to_all(outgoing, BOTH, split_axis=1, concat_axis=0, tiled=True)
    incoming = incoming.reshape(peer_count, rep_count, rows_own, half_cols)
    partner_res, incoming = lax.optimization_barrier((partner_res, incoming))
    integral = lax.dynamic_index_in_dim(integrals, slot, axis=0, keepdims=False)
    integral = integral.reshape(tile_width, rep_count, half_cols)
    halves = jnp.einsum(
        "tric,arc->rtia", incoming, integral, preferred_element_type=jnp.float32
    ).astype(jnp.bfloat16)
    contribution = (halves[0].astype(jnp.float32) + halves[1].astype(jnp.float32)).astype(
        jnp.bfloat16
    )

    quarter = local_rows // 2
    pairs = contribution.reshape(2, peer_count // 2, blocks, 2, quarter, tile_width)
    pairs = pairs[0].astype(jnp.float32) - pairs[1].astype(jnp.float32)
    pairs = pairs.astype(jnp.bfloat16).transpose(2, 0, 1, 3, 4)
    chunk_rows = 16
    pairs = pairs.reshape(peer_count * rep_count, chunk_rows, quarter * tile_width // chunk_rows)
    arrived = lax.all_to_all(pairs, BOTH, split_axis=0, concat_axis=0, tiled=True)
    arrived = arrived.reshape(peer_count * rep_count, quarter, tile_width)

    tile_ids = jnp.arange(residual_in.shape[1], dtype=jnp.int32)
    weights = ((every_ab[:, None] == tile_ids[None, :]) & (every_allowed[:, None] == 1)).astype(
        jnp.bfloat16
    )
    ladder = jnp.einsum("qa,qrc->rac", weights, arrived, preferred_element_type=jnp.float32)

    to_partner = mirror % local_rows
    inverse = jnp.argsort(to_partner)
    res_a = jnp.where(upper, partner_res[quarter:], residual_in[:quarter])
    res_b = jnp.where(
        upper,
        jnp.take(residual_in, inverse[quarter:], axis=0, mode="clip"),
        jnp.take(partner_res, to_partner[:quarter], axis=0, mode="clip"),
    )
    diff = res_a.astype(jnp.float32) - res_b.astype(jnp.float32)
    value = (0.5 * (diff + ladder)).astype(jnp.bfloat16)
    partner_value = partner_2(value, "tile", peer_count.bit_length() - 2)
    by_lower = jnp.concatenate(
        [jnp.where(upper, partner_value, value), jnp.where(upper, value, partner_value)]
    )
    place = jnp.where(upper, to_partner, jnp.arange(local_rows))
    sign = jnp.where(upper, -1.0, 1.0).astype(jnp.bfloat16)
    return sign * jnp.take(by_lower, place, axis=0, mode="clip")


def solution(mesh):
    return jax.shard_map(
        per_device,
        mesh=mesh,
        in_specs=(
            P("tile", None, "rep"),
            P("tile", None, None),
            P("tile"),
            P("tile"),
            P("tile"),
            P(("tile", "rep")),
            P(("tile", "rep"), None, None),
        ),
        out_specs=P(("tile", "rep"), None, None),
        check_vma=False,
    )
```
